32 devices in a mesh: dp: 4 (over y, core), cells: 8 (over z, x).
Axes of the slice: x: 2, y: 2, z: 4, core: 2. Of those that a mesh axis runs over, the one named last changes fastest.
Arguments:
- sensitivity: float32 [8192, 12288], P('dp', 'cells'), may hold values from -0.0546875 to 0.0546875
- observed: float32 [8192, 256], P('dp'), may hold values from -6 to 6
- models: float32 [12288, 256], P('cells'), may hold values from -6 to 6
- neighbour_map: int32 [4, 768], replicated, may hold values from 0 to 767, as said below
- edge_mask: int32 [12288], P('cells'), may hold values 0 or 1
Outputs:
- updated: float32 [12288, 256], P('cells')
The draws below stay inside these ranges and needn't reach their ends.
Inputs may be any that keep to these rules, and one draw needn't show every extreme that they name: `neighbour_map`: each row k maps every cell of a periodic 32 by 24 plane grid, numbered in a drawn order, to its neighbour in one of the four grid directions; every row is a permutation.
All inputs are finite; a program needn't handle non-finite values. No bound on the sum of `edge_mask` on one device may be relied on, other than what follows from the above.
Results may differ from the reference program's by a relative error of at most 0.0001.
Values sent between devices are 32-bit elements; how exact they have to be, the bound alone decides.
A program may use at most 128 MiB of HBM per device.

```python
import jax
import jax.numpy as jnp
from jax import lax

NDATA = 8192
PX = 32
PY = 24
SOLS = 256
ITERS = 2
PLANE = 768
NCELL = 12288


def draw_neighbour_map(key, part):
    total = PX * PY
    labels = jax.random.permutation(jax.random.fold_in(key, 11), total).astype(jnp.int32)
    index = jnp.arange(total, dtype=jnp.int32)
    first = index // PY
    second = index % PY
    targets = [(first + 1) % PX * PY + second, (first + PX - 1) % PX * PY + second, first * PY + (second + 1) % PY, first * PY + (second + PY - 1) % PY]
    rows = []
    for target in targets:
        row = jnp.zeros((total,), jnp.int32).at[labels].set(labels[target])
        rows.append(row)
    return jnp.stack(rows, axis=0)


def set_ends(entries, stream_key, low, largest):
    longest = entries.shape.index(max(entries.shape))
    spots = []
    for shift in (0, 1):
        where = [jax.random.randint(jax.random.fold_in(stream_key, axis), (), 0, length) for axis, length in enumerate(entries.shape)]
        where[longest] = (where[longest] + shift) % entries.shape[longest]
        spots.append(tuple(where))
    return entries.at[spots[0]].set(low).at[spots[1]].set(largest)


def level_of(own_key, shape, shards, least, high):
    def one(dim, parts):
        steps = jax.random.uniform(jax.random.fold_in(jax.random.fold_in(own_key, 6), dim), (parts,), jnp.float32, least / len(shards), high / len(shards))
        return jnp.repeat(jnp.exp(steps), shape[dim] // parts).reshape((-1,) + (1,) * (len(shape) - dim - 1))

    factor_of = one(*shards[0])
    for cut in shards[1:]:
        factor_of = factor_of * one(*cut)
    return factor_of


def centred(rng, shape, spread, most, shards=(), kind=jnp.bfloat16):
    values = jax.random.normal(rng, shape, jnp.float32) * spread
    if len(shards) > 0:
        values = level_of(rng, shape, shards, -0.22, 0.18) * values
    return jnp.clip(values, min=-most, max=most).astype(kind)


def setup_inputs(seed: int = 0) -> dict:
    key_of = jax.random.split(jax.random.key(seed), 6)
    return {
        "sensitivity": centred(key_of[0], (NDATA, NCELL), NCELL ** -0.5, 0.0546875, ((0, 4), (1, 8)), jnp.float32),
        "observed": centred(key_of[1], (NDATA, SOLS), 1.0, 6.0, ((0, 4),), jnp.float32),
        "models": centred(key_of[2], (NCELL, SOLS), 1.0, 6.0, ((0, 8),), jnp.float32),
        "neighbour_map": draw_neighbour_map(jax.random.fold_in(key_of[5], 71), 0),
        "edge_mask": set_ends((jax.random.randint(key_of[4], (NCELL,), 0, 4) < 1).astype(jnp.int32), jax.random.fold_in(key_of[4], 1), 0, 1),
    }


def smooth_all(current, neighbour_map, edge_mask):
    count = current.shape[0] // PLANE
    planes = current.reshape(count, PLANE, current.shape[1])
    zero_plane = jnp.zeros((1, PLANE, current.shape[1]), jnp.float32)
    above = jnp.concatenate([zero_plane, planes[:-1]], axis=0)
    below = jnp.concatenate([planes[1:], zero_plane], axis=0)
    total = jnp.zeros_like(planes)
    for other in (above, below):
        diff = other - planes
        total = total + diff / jnp.sqrt(1.0 + diff * diff)
    for k in range(4):
        other = jnp.take(planes, neighbour_map[k], axis=1)
        diff = other - planes
        total = total + diff / jnp.sqrt(1.0 + diff * diff)
    scale = 1.0 - 0.75 * edge_mask.astype(jnp.float32).reshape(count, PLANE, 1)
    return (total * scale).reshape(current.shape)

def reference(sensitivity, observed, models, neighbour_map, edge_mask):
    current = models
    for step in range(ITERS):
        predicted = jnp.dot(sensitivity, current, precision=lax.Precision.HIGHEST, preferred_element_type=jnp.float32)
        misfit = predicted - observed
        weighted = misfit / jnp.maximum(jnp.abs(misfit), 1.0)
        gradient = lax.dot_general(sensitivity, weighted, (((0,), (0,)), ((), ())), precision=lax.Precision.HIGHEST, preferred_element_type=jnp.float32)
        current = current - 1.0 * gradient + 0.05 * smooth_all(current, neighbour_map, edge_mask)
    return current
```

```python
import functools

import jax
import jax.numpy as jnp
from jax import lax
from jax.experimental import pallas as pl
from jax.experimental.pallas import tpu as pltpu
from jax.sharding import PartitionSpec as P

ITERS = 2
CHUNK = 128
PARTS = 2
F32 = jnp.float32
BF16 = jnp.bfloat16


def split(x):
    hi = x.astype(BF16)
    return hi, (x - hi.astype(F32)).astype(BF16)


def bits_of(count):
    return count.bit_length() - 1


def dot(a, b, dims):
    return lax.dot_general(a, b, (dims, ((), ())), preferred_element_type=F32)


def aligned(start, size):
    return pl.ds(pl.multiple_of(start, 8), size)


class Halving:
    def __init__(self, axis, count, rows, sends, recvs):
        self.axis, self.rows = axis, rows
        self.bits = bits_of(count)
        self.sends, self.recvs = sends, recvs
        me = lax.axis_index(axis)
        self.bit = [(me // 2**b) % 2 for b in range(self.bits)]
        self.partner = [me + (1 - 2 * self.bit[b]) * 2**b for b in range(self.bits)]
        self.off, self.size = [0], [rows]
        for b in range(self.bits):
            half = self.size[b] // 2
            self.off.append(self.off[b] + self.bit[b] * half)
            self.size.append(half)

    def reduce(self, data, land, chunk, b):
        half = self.size[b + 1]
        away = self.off[b] + (1 - self.bit[b]) * half
        return pltpu.make_async_remote_copy(
            src_ref=data.at[aligned(chunk * self.rows + away, half)],
            dst_ref=land.at[aligned(chunk * self.rows + self.rows - self.size[b], half)],
            send_sem=self.sends.at[b, chunk],
            recv_sem=self.recvs.at[b, chunk],
            device_id={self.axis: self.partner[b]},
            device_id_type=pl.DeviceIdType.MESH,
        )

    def kept(self, chunk, b):
        return aligned(chunk * self.rows + self.off[b + 1], self.size[b + 1])

    def landed(self, chunk, b):
        return aligned(chunk * self.rows + self.rows - self.size[b], self.size[b + 1])

    def gather(self, data, chunk, b):
        here = data.at[self.kept(chunk, b)]
        return pltpu.make_async_remote_copy(
            src_ref=here,
            dst_ref=here,
            send_sem=self.sends.at[self.bits + b, chunk],
            recv_sem=self.recvs.at[self.bits + b, chunk],
            device_id={self.axis: self.partner[b]},
            device_id_type=pl.DeviceIdType.MESH,
        )

    def stage(self, s, chunk, data, land, result, finish):
        bits = self.bits
        if s > 0 and s <= bits:
            self.reduce(data, land, chunk, s - 1).wait()
            kept = self.kept(chunk, s - 1)
            total = data[kept, :] + land[self.landed(chunk, s - 1), :]
            if s < bits:
                data[kept, :] = total
            else:
                finish(chunk, kept, total)
        elif s > bits:
            self.gather(result, chunk, 2 * bits - s).wait()
        if s < bits:
            self.reduce(data, land, chunk, s).start()
        elif s < 2 * bits:
            self.gather(result, chunk, 2 * bits - 1 - s).start()


def body(sizes, plane, sens_hbm, obs_ref, models_ref, near_ref, mask_ref, out_ref,
         sens, part, land, weighted, grad, gland, middle, high, low, smooth,
         under, over, load_sem, c_send, c_recv, d_send, d_recv, h_send, h_recv):
    n_dp, n_cells = sizes
    ndata, ncell = sens.shape
    me = lax.axis_index("cells")
    rows = part.shape[0] // c_send.shape[1]
    chunks = ndata // rows
    parts = d_send.shape[1]
    prow = ncell // parts
    per_plane = plane // prow
    cells = Halving("cells", n_cells, rows, c_send, c_recv)
    dp = Halving("dp", n_dp, prow, d_send, d_recv)
    seg = dp.size[-1]
    own = dp.off[-1]

    def load(c):
        at = aligned(c * rows, rows)
        return pltpu.make_async_copy(sens_hbm.at[at], sens.at[at], load_sem.at[c])

    for c in range(chunks):
        load(c).start()

    barrier = pltpu.get_barrier_semaphore()

    def greet(where):
        pl.semaphore_signal(barrier, inc=1, device_id=where, device_id_type=pl.DeviceIdType.MESH)

    for b in range(cells.bits):
        greet({"cells": cells.partner[b]})
    for b in range(dp.bits):
        greet({"dp": dp.partner[b]})

    has_under, has_over = me > 0, me < n_cells - 1

    @pl.when(has_under)
    def _():
        greet({"cells": me - 1})

    @pl.when(has_over)
    def _():
        greet({"cells": me + 1})

    @pl.when(me == 0)
    def _():
        under[...] = jnp.zeros_like(under)

    @pl.when(me == n_cells - 1)
    def _():
        over[...] = jnp.zeros_like(over)

    pl.semaphore_wait(
        barrier,
        cells.bits + dp.bits + (me + n_cells - 1) // n_cells + (2 * n_cells - 2 - me) // n_cells,
    )

    states = [models_ref] + [middle] * (ITERS - 1) + [out_ref]

    def halo(current, step, i, upward):
        source = (ncell - plane if upward else 0) + i * prow + own
        return pltpu.make_async_remote_copy(
            src_ref=current.at[aligned(source, seg)],
            dst_ref=(under if upward else over).at[step, pl.ds(i * seg, seg)],
            send_sem=h_send.at[step, int(upward), i],
            recv_sem=h_recv.at[step, int(upward), i],
            device_id={"cells": me + 1 if upward else me - 1},
            device_id_type=pl.DeviceIdType.MESH,
        )

    def halos(current, step, act_over, act_under):
        @pl.when(has_over)
        def _():
            for i in range(per_plane):
                act_over(i)

        @pl.when(has_under)
        def _():
            for i in range(per_plane):
                act_under(i)

    for step in range(ITERS):
        current, later = states[step], states[step + 1]

        halos(
            current, step,
            lambda i: halo(current, step, i, True).start(),
            lambda i: halo(current, step, i, False).start(),
        )
        hi, lo = split(current[...])
        high[...] = hi
        low[...] = lo
        grad[...] = jnp.zeros_like(grad)

        def predict(c):
            at = aligned(c * rows, rows)
            if step == 0:
                load(c).wait()
            s_hi, s_lo = split(sens[at, :])
            nn = ((1,), (0,))
            part[at, :] = dot(s_hi, high[...], nn) + dot(s_hi, low[...], nn) + dot(s_lo, high[...], nn)

        def reweight(c, kept, total):
            misfit = total - obs_ref[kept, :]
            weighted[kept, :] = misfit / jnp.maximum(jnp.abs(misfit), 1.0)

        def back(c):
            at = aligned(c * rows, rows)
            s_hi, s_lo = split(sens[at, :])
            w_hi, w_lo = split(weighted[at, :])
            tn = ((0,), (0,))
            grad[...] += dot(s_hi, w_hi, tn) + dot(s_hi, w_lo, tn) + dot(s_lo, w_hi, tn)

        def smooth_part(q):
            base = q * prow + own
            inner = lax.rem(base, plane)
            first = base - inner
            cell = current[aligned(base, seg), :]
            total = jnp.zeros_like(cell)

            def add(other):
                diff = other - cell
                return diff / jnp.sqrt(1.0 + diff * diff)

            at = aligned(lax.rem(q, per_plane) * seg, seg)
            below = current[aligned(jnp.maximum(base - plane, 0), seg), :]
            above = current[aligned(jnp.minimum(base + plane, ncell - seg), seg), :]
            total += add(jnp.where(first == 0, under[step, at, :], below))
            total += add(jnp.where(first == ncell - plane, over[step, at, :], above))
            whole = pl.ds(pl.multiple_of(first, 16), plane)
            nn = ((1,), (0,))
            for k in range(4):
                column = near_ref[aligned(inner, seg), k:k + 1]
                pick = column == lax.broadcasted_iota(jnp.int32, (seg, plane), 1)
                pick = jnp.where(pick, 1.0, 0.0).astype(BF16)
                total += add(dot(pick, high[whole, :], nn) + dot(pick, low[whole, :], nn))
            scale = 1.0 - 0.75 * mask_ref[aligned(base, seg), :].astype(F32)
            smooth[aligned(q * seg, seg), :] = total * scale

        predict(0)
        stages = 2 * cells.bits

        def slot(t, carry):
            for s in reversed(range(stages + 1)):
                c = t - s

                @pl.when(jnp.logical_and(c >= 0, c < chunks))
                def _():
                    cells.stage(s, c, part, land, weighted, reweight)

            @pl.when(t + 1 < chunks)
            def _():
                predict(t + 1)

            q = t - 3

            @pl.when(q == 0)
            def _():
                halos(
                    current, step,
                    lambda i: halo(current, step, i, True).wait_send(),
                    lambda i: halo(current, step, i, False).wait_send(),
                )
                halos(
                    current, step,
                    lambda i: halo(current, step, i, False).wait_recv(),
                    lambda i: halo(current, step, i, True).wait_recv(),
                )

            @pl.when(jnp.logical_and(q >= 0, q < parts))
            def _():
                smooth_part(q)

            @pl.when(t >= stages)
            def _():
                back(t - stages)

            return carry

        lax.fori_loop(0, chunks + stages, slot, 0)

        def update(q, kept, total):
            later[kept, :] = current[kept, :] - 1.0 * total + 0.05 * smooth[aligned(q * seg, seg), :]

        def dp_slot(t, carry):
            for s in reversed(range(2 * dp.bits + 1)):
                q = t - s

                @pl.when(jnp.logical_and(q >= 0, q < parts))
                def _():
                    dp.stage(s, q, grad, gland, later, update)

            return carry

        lax.fori_loop(0, parts + 2 * dp.bits, dp_slot, 0)


def invert(n_dp, n_cells, sensitivity, observed, models, neighbour_map, edge_mask):
    ndata, ncell = sensitivity.shape
    sols = models.shape[1]
    plane = neighbour_map.shape[1]
    rows = max(CHUNK, 8 * n_cells)
    chunks = ndata // rows
    parts = ncell // plane * PARTS
    seg = ncell // parts // n_dp
    vmem = pl.BlockSpec(memory_space=pltpu.VMEM)
    dma = pltpu.SemaphoreType.DMA
    nb, nd = 2 * bits_of(n_cells), 2 * bits_of(n_dp)
    return pl.pallas_call(
        functools.partial(body, (n_dp, n_cells), plane),
        out_shape=jax.ShapeDtypeStruct((ncell, sols), F32),
        in_specs=[pl.BlockSpec(memory_space=pl.ANY)] + [vmem] * 4,
        out_specs=vmem,
        scratch_shapes=[
            pltpu.VMEM((ndata, ncell), F32),
            pltpu.VMEM((ndata, sols), F32),
            pltpu.VMEM((ndata, sols), F32),
            pltpu.VMEM((ndata, sols), F32),
            pltpu.VMEM((ncell, sols), F32),
            pltpu.VMEM((ncell, sols), F32),
            pltpu.VMEM((ncell, sols), F32),
            pltpu.VMEM((ncell, sols), BF16),
            pltpu.VMEM((ncell, sols), BF16),
            pltpu.VMEM((parts * seg, sols), F32),
            pltpu.VMEM((ITERS, PARTS * seg, sols), F32),
            pltpu.VMEM((ITERS, PARTS * seg, sols), F32),
            dma((chunks,)),
            dma((nb, chunks)),
            dma((nb, chunks)),
            dma((nd, parts)),
            dma((nd, parts)),
            dma((ITERS, 2, PARTS)),
            dma((ITERS, 2, PARTS)),
        ],
        compiler_params=pltpu.CompilerParams(
            collective_id=0, has_side_effects=True, vmem_limit_bytes=60 * 1024 * 1024
        ),
        name="invert",
    )(sensitivity, observed, models, neighbour_map.T, edge_mask[:, None])


def solution(mesh):
    return jax.shard_map(
        functools.partial(invert, mesh.shape["dp"], mesh.shape["cells"]),
        mesh=mesh,
        in_specs=(P("dp", "cells"), P("dp", None), P("cells", None), P(), P("cells")),
        out_specs=P("cells", None),
        check_vma=False,
    )
```

```python
import functools

import jax
import jax.numpy as jnp
from jax import lax
from jax.experimental import pallas as pl
from jax.experimental.pallas import tpu as pltpu
from jax.sharding import PartitionSpec as P

ITERS = 2
CHUNK = 256
PARTS = 1
HALVES = 2
F32 = jnp.float32
BF16 = jnp.bfloat16


def split(x):
    hi = x.astype(BF16)
    return hi, (x - hi.astype(F32)).astype(BF16)


def digits_of(count, first):
    digits = []
    while count > 1:
        digits.append(first if not digits else min(4, count))
        count //= digits[-1]
    return digits


def radix(n_dp, n_cells):
    return digits_of(n_dp, 2), digits_of(n_cells, 2)


def dot(a, b, dims):
    return lax.dot_general(a, b, (dims, ((), ())), preferred_element_type=F32)


def aligned(start, size):
    return pl.ds(pl.multiple_of(start, 8), size)


class Scatter:
    def __init__(self, axis, digits, rows, sends, recvs):
        self.axis, self.rows, self.digits = axis, rows, digits
        self.sends, self.recvs = sends, recvs
        self.levels = len(digits)
        self.stages = 2 * self.levels
        me = lax.axis_index(axis)
        self.peer, self.away, self.off, self.size, self.sem = [], [], [0], [rows], []
        stride, sem = 1, 0
        for b, base in enumerate(digits):
            mine = (me // stride) % base
            piece = self.size[b] // base
            others = [(mine + j) % base for j in range(1, base)]
            self.peer.append([me + (v - mine) * stride for v in others])
            self.away.append([self.off[b] + v * piece for v in others])
            self.off.append(self.off[b] + mine * piece)
            self.size.append(piece)
            self.sem.append(sem)
            sem += base - 1
            stride *= base
        self.copies = sem

    def kept(self, chunk, b):
        return aligned(chunk * self.rows + self.off[b + 1], self.size[b + 1])

    def landed(self, chunk, b, j):
        at = self.rows - self.size[b] + j * self.size[b + 1]
        return aligned(chunk * self.rows + at, self.size[b + 1])

    def remote(self, source, target, slot, sem, peer):
        return pltpu.make_async_remote_copy(
            src_ref=source,
            dst_ref=target,
            send_sem=self.sends.at[sem, slot],
            recv_sem=self.recvs.at[sem, slot],
            device_id={self.axis: peer},
            device_id_type=pl.DeviceIdType.MESH,
        )

    def reduces(self, data, land, chunk, slot, b):
        for j in range(self.digits[b] - 1):
            source = data.at[aligned(chunk * self.rows + self.away[b][j], self.size[b + 1])]
            target = land.at[self.landed(chunk, b, j)]
            yield self.remote(source, target, slot, self.sem[b] + j, self.peer[b][j])

    def gathers(self, data, chunk, slot, b):
        here = data.at[self.kept(chunk, b)]
        for j in range(self.digits[b] - 1):
            yield self.remote(here, here, slot, self.copies + self.sem[b] + j, self.peer[b][j])

    def stage(self, s, chunk, slot, data, land, result, finish):
        levels = self.levels
        if 0 < s <= levels:
            b = s - 1
            for copy in self.reduces(data, land, chunk, slot, b):
                copy.wait()
            kept = self.kept(chunk, b)
            total = data[kept, :]
            for j in range(self.digits[b] - 1):
                total += land[self.landed(chunk, b, j), :]
            if s < levels:
                data[kept, :] = total
            else:
                finish(kept, total)
        elif s > levels:
            for copy in self.gathers(result, chunk, slot, 2 * levels - s):
                copy.wait()
        if s < levels:
            for copy in self.reduces(data, land, chunk, slot, s):
                copy.start()
        elif s < 2 * levels:
            for copy in self.gathers(result, chunk, slot, 2 * levels - 1 - s):
                copy.start()


def body(sizes, plane, sens_hbm, obs_hbm, models_hbm, near_ref, mask_ref, out_hbm,
         sens, obs, part, land, weighted, grad, gland, state, high, low, smooth,
         under, over, load_sem, obs_sem, edge_sem, c_send, c_recv, d_send, d_recv, h_send, h_recv):
    n_dp, n_cells = sizes
    ndata, ncell = sens.shape
    halves, _, width = grad.shape
    me = lax.axis_index("cells")
    chunks = c_send.shape[1] // halves
    rows = ndata // chunks
    parts = d_send.shape[1] // halves
    prow = ncell // parts
    per_plane = plane // prow
    dp_digits, cell_digits = radix(n_dp, n_cells)
    cells = Scatter("cells", cell_digits, rows, c_send, c_recv)
    dp = Scatter("dp", dp_digits, prow, d_send, d_recv)
    seg = dp.size[-1]
    own = dp.off[-1]
    units = halves * chunks
    delay = chunks + cells.stages
    period = delay + parts + dp.stages
    slots = (ITERS - 1) * period + delay + units - chunks + parts + dp.stages
    nn, tn = ((1,), (0,)), ((0,), (0,))

    def load(c):
        at = aligned(c * rows, rows)
        return pltpu.make_async_copy(sens_hbm.at[at], sens.at[at], load_sem.at[c])

    def columns(h):
        return pl.ds(h * width, width)

    def enter(h):
        return pltpu.make_async_copy(models_hbm.at[:, columns(h)], state.at[0, h], edge_sem.at[h])

    def leave(h):
        return pltpu.make_async_copy(state.at[ITERS, h], out_hbm.at[:, columns(h)], edge_sem.at[h])

    def watch(h):
        return pltpu.make_async_copy(obs_hbm.at[:, columns(h)], obs.at[h], obs_sem.at[h])

    for h in range(halves):
        enter(h).start()
    for c in range(chunks):
        load(c).start()
    for h in range(halves):
        watch(h).start()

    barrier = pltpu.get_barrier_semaphore()

    def greet(where):
        pl.semaphore_signal(barrier, inc=1, device_id=where, device_id_type=pl.DeviceIdType.MESH)

    for peers in cells.peer:
        for peer in peers:
            greet({"cells": peer})
    for peers in dp.peer:
        for peer in peers:
            greet({"dp": peer})

    has_under, has_over = me > 0, me < n_cells - 1

    @pl.when(has_under)
    def _():
        greet({"cells": me - 1})

    @pl.when(has_over)
    def _():
        greet({"cells": me + 1})

    @pl.when(me == 0)
    def _():
        under[...] = jnp.zeros_like(under)

    @pl.when(me == n_cells - 1)
    def _():
        over[...] = jnp.zeros_like(over)

    for h in range(halves):
        enter(h).wait()

    pl.semaphore_wait(
        barrier,
        cells.copies + dp.copies + (me + n_cells - 1) // n_cells + (2 * n_cells - 2 - me) // n_cells,
    )

    def halo(step, h, i, upward):
        source = (ncell - plane if upward else 0) + i * prow + own
        return pltpu.make_async_remote_copy(
            src_ref=state.at[step, h, aligned(source, seg)],
            dst_ref=(under if upward else over).at[step, h, pl.ds(i * seg, seg)],
            send_sem=h_send.at[step, h, int(upward) * per_plane + i],
            recv_sem=h_recv.at[step, h, int(upward) * per_plane + i],
            device_id={"cells": me + 1 if upward else me - 1},
            device_id_type=pl.DeviceIdType.MESH,
        )

    def halos(act_over, act_under):
        @pl.when(has_over)
        def _():
            for i in range(per_plane):
                act_over(i)

        @pl.when(has_under)
        def _():
            for i in range(per_plane):
                act_under(i)

    def predict(step, h, c):
        @pl.when(c == 0)
        def _():
            halos(
                lambda i: halo(step, h, i, True).start(),
                lambda i: halo(step, h, i, False).start(),
            )
            hi, lo = split(state[step, h])
            high[h] = hi
            low[h] = lo

        @pl.when(jnp.logical_and(step == 0, h == 0))
        def _():
            load(c).wait()

        at = aligned(c * rows, rows)
        s_hi, s_lo = split(sens[at, :])
        part[h, at, :] = dot(s_hi, high[h], nn) + dot(s_hi, low[h], nn) + dot(s_lo, high[h], nn)

    def back(step, h, c):
        @pl.when(c == 0)
        def _():
            grad[h] = jnp.zeros_like(grad[h])

        at = aligned(c * rows, rows)
        s_hi, s_lo = split(sens[at, :])
        w_hi, w_lo = split(weighted[h, at, :])
        grad[h] += dot(s_hi, w_hi, tn) + dot(s_hi, w_lo, tn) + dot(s_lo, w_hi, tn)

    def smooth_part(step, h, q):
        @pl.when(q == 0)
        def _():
            halos(
                lambda i: halo(step, h, i, True).wait_send(),
                lambda i: halo(step, h, i, False).wait_send(),
            )
            halos(
                lambda i: halo(step, h, i, False).wait_recv(),
                lambda i: halo(step, h, i, True).wait_recv(),
            )

        base = q * prow + own
        inner = lax.rem(base, plane)
        first = base - inner
        cell = state[step, h, aligned(base, seg), :]
        total = jnp.zeros_like(cell)

        def add(other):
            diff = other - cell
            return diff / jnp.sqrt(1.0 + diff * diff)

        at = aligned(lax.rem(q, per_plane) * seg, seg)
        below = state[step, h, aligned(jnp.maximum(base - plane, 0), seg), :]
        above = state[step, h, aligned(jnp.minimum(base + plane, ncell - seg), seg), :]
        total += add(jnp.where(first == 0, under[step, h, at, :], below))
        total += add(jnp.where(first == ncell - plane, over[step, h, at, :], above))
        whole = pl.ds(pl.multiple_of(first, 16), plane)
        for k in range(4):
            column = near_ref[aligned(inner, seg), k:k + 1]
            pick = column == lax.broadcasted_iota(jnp.int32, (seg, plane), 1)
            pick = jnp.where(pick, 1.0, 0.0).astype(BF16)
            total += add(dot(pick, high[h, whole, :], nn) + dot(pick, low[h, whole, :], nn))
        scale = 1.0 - 0.75 * mask_ref[aligned(base, seg), :].astype(F32)
        smooth[h, aligned(q * seg, seg), :] = total * scale

    def at_slot(x, count, act):
        step, unit = lax.div(x, period), lax.rem(x, period)
        h, index = lax.div(unit, chunks), lax.rem(unit, chunks)

        @pl.when((x >= 0) & (step < ITERS) & (unit < units) & (index < count))
        def _():
            act(step, h, index)

    def cell_stage(s, step, h, c):
        def reweight(kept, total):
            misfit = total - obs[h, kept, :]
            weighted[h, kept, :] = misfit / jnp.maximum(jnp.abs(misfit), 1.0)

        cells.stage(s, c, h * chunks + c, part.at[h], land.at[h], weighted.at[h], reweight)

    def dp_stage(s, step, h, q):
        def update(kept, total):
            moved = state[step, h, kept, :] - 1.0 * total
            state[step + 1, h, kept, :] = moved + 0.05 * smooth[h, aligned(q * seg, seg), :]

        dp.stage(s, q, h * parts + q, grad.at[h], gland.at[h], state.at[step + 1, h], update)

    def slot(t, carry):
        @pl.when(t == 0)
        def _():
            for h in range(halves):
                watch(h).wait()

        for s in reversed(range(cells.stages + 1)):
            at_slot(t - s, chunks, functools.partial(cell_stage, s))
        for s in reversed(range(dp.stages + 1)):
            at_slot(t - delay - s, parts, functools.partial(dp_stage, s))
        at_slot(t + 1, chunks, predict)
        at_slot(t - 2, parts, smooth_part)
        at_slot(t - cells.stages, chunks, back)
        return carry

    lax.fori_loop(-1, slots, slot, 0)
    for h in range(halves):
        leave(h).start()
    for h in range(halves):
        leave(h).wait()


def invert(n_dp, n_cells, sensitivity, observed, models, neighbour_map, edge_mask):
    ndata, ncell = sensitivity.shape
    width = models.shape[1] // HALVES
    plane = neighbour_map.shape[1]
    rows = max(CHUNK, 8 * n_cells)
    chunks = ndata // rows
    parts = ncell // plane * PARTS
    seg = ncell // parts // n_dp
    vmem = pl.BlockSpec(memory_space=pltpu.VMEM)
    hbm = pl.BlockSpec(memory_space=pl.ANY)
    dma = pltpu.SemaphoreType.DMA
    nd, nb = (2 * sum(d - 1 for d in digits) for digits in radix(n_dp, n_cells))
    return pl.pallas_call(
        functools.partial(body, (n_dp, n_cells), plane),
        out_shape=jax.ShapeDtypeStruct(models.shape, F32),
        in_specs=[hbm] * 3 + [vmem] * 2,
        out_specs=hbm,
        scratch_shapes=[
            pltpu.VMEM((ndata, ncell), F32),
            pltpu.VMEM((HALVES, ndata, width), F32),
            pltpu.VMEM((HALVES, ndata, width), F32),
            pltpu.VMEM((HALVES, ndata, width), F32),
            pltpu.VMEM((HALVES, ndata, width), F32),
            pltpu.VMEM((HALVES, ncell, width), F32),
            pltpu.VMEM((HALVES, ncell, width), F32),
            pltpu.VMEM((ITERS + 1, HALVES, ncell, width), F32),
            pltpu.VMEM((HALVES, ncell, width), BF16),
            pltpu.VMEM((HALVES, ncell, width), BF16),
            pltpu.VMEM((HALVES, parts * seg, width), F32),
            pltpu.VMEM((ITERS, HALVES, PARTS * seg, width), F32),
            pltpu.VMEM((ITERS, HALVES, PARTS * seg, width), F32),
            dma((chunks,)),
            dma((HALVES,)),
            dma((HALVES,)),
            dma((nb, HALVES * chunks)),
            dma((nb, HALVES * chunks)),
            dma((nd, HALVES * parts)),
            dma((nd, HALVES * parts)),
            dma((ITERS, HALVES, 2 * PARTS)),
            dma((ITERS, HALVES, 2 * PARTS)),
        ],
        compiler_params=pltpu.CompilerParams(
            collective_id=0, has_side_effects=True, vmem_limit_bytes=60 * 1024 * 1024
        ),
        name="invert",
    )(sensitivity, observed, models, neighbour_map.T, edge_mask[:, None])


def solution(mesh):
    return jax.shard_map(
        functools.partial(invert, mesh.shape["dp"], mesh.shape["cells"]),
        mesh=mesh,
        in_specs=(P("dp", "cells"), P("dp", None), P("cells", None), P(), P("cells")),
        out_specs=P("cells", None),
        check_vma=False,
    )
```

```python
import functools

import jax
import jax.numpy as jnp
from jax import lax
from jax.experimental import pallas as pl
from jax.experimental.pallas import tpu as pltpu
from jax.sharding import PartitionSpec as P

ITERS = 2
CHUNK = 256
PARTS = 1
HALVES = 2
LAG = 3
DP_LAG = 3
RADIX = 2
F32 = jnp.float32
BF16 = jnp.bfloat16


def split(x):
    hi = x.astype(BF16)
    return hi, (x - hi.astype(F32)).astype(BF16)


def digits_of(count, first):
    digits = []
    while count > 1:
        digits.append(first if not digits else min(RADIX, count))
        count //= digits[-1]
    return digits


def radix(n_dp, n_cells):
    return digits_of(n_dp, 2), digits_of(n_cells, 2)


def dot(a, b, dims):
    return lax.dot_general(a, b, (dims, ((), ())), preferred_element_type=F32)


def aligned(start, size):
    return pl.ds(pl.multiple_of(start, 8), size)


class Scatter:
    def __init__(self, axis, digits, rows, sends, recvs):
        self.axis, self.rows, self.digits = axis, rows, digits
        self.sends, self.recvs = sends, recvs
        self.levels = len(digits)
        self.stages = 2 * self.levels
        me = lax.axis_index(axis)
        self.peer, self.away, self.off, self.size, self.sem = [], [], [0], [rows], []
        stride, sem = 1, 0
        for b, base in enumerate(digits):
            mine = (me // stride) % base
            piece = self.size[b] // base
            others = [(mine + j) % base for j in range(1, base)]
            self.peer.append([me + (v - mine) * stride for v in others])
            self.away.append([self.off[b] + v * piece for v in others])
            self.off.append(self.off[b] + mine * piece)
            self.size.append(piece)
            self.sem.append(sem)
            sem += base - 1
            stride *= base
        self.copies = sem

    def kept(self, chunk, b):
        return aligned(chunk * self.rows + self.off[b + 1], self.size[b + 1])

    def landed(self, chunk, b, j):
        at = self.rows - self.size[b] + j * self.size[b + 1]
        return aligned(chunk * self.rows + at, self.size[b + 1])

    def remote(self, source, target, slot, sem, peer):
        return pltpu.make_async_remote_copy(
            src_ref=source,
            dst_ref=target,
            send_sem=self.sends.at[sem, slot],
            recv_sem=self.recvs.at[sem, slot],
            device_id={self.axis: peer},
            device_id_type=pl.DeviceIdType.MESH,
        )

    def reduces(self, data, land, chunk, slot, b):
        for j in range(self.digits[b] - 1):
            source = data.at[aligned(chunk * self.rows + self.away[b][j], self.size[b + 1])]
            target = land.at[self.landed(chunk, b, j)]
            yield self.remote(source, target, slot, self.sem[b] + j, self.peer[b][j])

    def gathers(self, data, chunk, slot, b):
        here = data.at[self.kept(chunk, b)]
        for j in range(self.digits[b] - 1):
            yield self.remote(here, here, slot, self.copies + self.sem[b] + j, self.peer[b][j])

    def stage(self, s, chunk, slot, data, land, result, finish):
        levels = self.levels
        if 0 < s <= levels:
            b = s - 1
            for copy in self.reduces(data, land, chunk, slot, b):
                copy.wait()
            kept = self.kept(chunk, b)
            total = data[kept, :]
            for j in range(self.digits[b] - 1):
                total += land[self.landed(chunk, b, j), :]
            if s < levels:
                data[kept, :] = total
            else:
                finish(kept, total)
        elif s > levels:
            for copy in self.gathers(result, chunk, slot, 2 * levels - s):
                copy.wait()
        if s < levels:
            for copy in self.reduces(data, land, chunk, slot, s):
                copy.start()
        elif s < 2 * levels:
            for copy in self.gathers(result, chunk, slot, 2 * levels - 1 - s):
                copy.start()


def body(sizes, plane, sens_hbm, obs_hbm, models_hbm, near_ref, mask_ref, out_hbm,
         sens, obs, part, land, weighted, grad, gland, state, high, low, smooth,
         under, over, load_sem, obs_sem, edge_sem, c_send, c_recv, d_send, d_recv, h_send, h_recv):
    n_dp, n_cells = sizes
    ndata, ncell = sens.shape
    halves, _, width = grad.shape
    me = lax.axis_index("cells")
    chunks = c_send.shape[1] // halves
    rows = ndata // chunks
    parts = d_send.shape[1] // halves
    prow = ncell // parts
    per_plane = plane // prow
    dp_digits, cell_digits = radix(n_dp, n_cells)
    cells = Scatter("cells", cell_digits, rows, c_send, c_recv)
    dp = Scatter("dp", dp_digits, prow, d_send, d_recv)
    seg = dp.size[-1]
    own = dp.off[-1]
    units = halves * chunks
    delay = chunks + LAG * cells.stages
    period = delay + parts + DP_LAG * dp.stages
    slots = (ITERS - 1) * period + delay + units - chunks + parts + DP_LAG * dp.stages
    nn, tn = ((1,), (0,)), ((0,), (0,))

    def load(c):
        at = aligned(c * rows, rows)
        return pltpu.make_async_copy(sens_hbm.at[at], sens.at[at], load_sem.at[c])

    def columns(h):
        return pl.ds(h * width, width)

    def enter(h):
        return pltpu.make_async_copy(models_hbm.at[:, columns(h)], state.at[0, h], edge_sem.at[h])

    def leave(h):
        return pltpu.make_async_copy(state.at[ITERS, h], out_hbm.at[:, columns(h)], edge_sem.at[h])

    def watch(h):
        return pltpu.make_async_copy(obs_hbm.at[:, columns(h)], obs.at[h], obs_sem.at[h])

    for h in range(halves):
        enter(h).start()
    for c in range(chunks):
        load(c).start()
    for h in range(halves):
        watch(h).start()

    barrier = pltpu.get_barrier_semaphore()

    def greet(where):
        pl.semaphore_signal(barrier, inc=1, device_id=where, device_id_type=pl.DeviceIdType.MESH)

    for peers in cells.peer:
        for peer in peers:
            greet({"cells": peer})
    for peers in dp.peer:
        for peer in peers:
            greet({"dp": peer})

    has_under, has_over = me > 0, me < n_cells - 1

    @pl.when(has_under)
    def _():
        greet({"cells": me - 1})

    @pl.when(has_over)
    def _():
        greet({"cells": me + 1})

    @pl.when(me == 0)
    def _():
        under[...] = jnp.zeros_like(under)

    @pl.when(me == n_cells - 1)
    def _():
        over[...] = jnp.zeros_like(over)

    for h in range(halves):
        enter(h).wait()

    pl.semaphore_wait(
        barrier,
        cells.copies + dp.copies + (me + n_cells - 1) // n_cells + (2 * n_cells - 2 - me) // n_cells,
    )

    def halo(step, h, i, upward):
        source = (ncell - plane if upward else 0) + i * prow + own
        return pltpu.make_async_remote_copy(
            src_ref=state.at[step, h, aligned(source, seg)],
            dst_ref=(under if upward else over).at[step, h, pl.ds(i * seg, seg)],
            send_sem=h_send.at[step, h, int(upward) * per_plane + i],
            recv_sem=h_recv.at[step, h, int(upward) * per_plane + i],
            device_id={"cells": me + 1 if upward else me - 1},
            device_id_type=pl.DeviceIdType.MESH,
        )

    def halos(act_over, act_under):
        @pl.when(has_over)
        def _():
            for i in range(per_plane):
                act_over(i)

        @pl.when(has_under)
        def _():
            for i in range(per_plane):
                act_under(i)

    def predict(step, h, c):
        @pl.when(c == 0)
        def _():
            halos(
                lambda i: halo(step, h, i, True).start(),
                lambda i: halo(step, h, i, False).start(),
            )
            hi, lo = split(state[step, h])
            high[h] = hi
            low[h] = lo

        @pl.when(jnp.logical_and(step == 0, h == 0))
        def _():
            load(c).wait()

        at = aligned(c * rows, rows)
        s_hi, s_lo = split(sens[at, :])
        part[h, at, :] = dot(s_hi, high[h], nn) + dot(s_hi, low[h], nn) + dot(s_lo, high[h], nn)

    def back(step, h, c):
        @pl.when(c == 0)
        def _():
            grad[h] = jnp.zeros_like(grad[h])

        at = aligned(c * rows, rows)
        s_hi, s_lo = split(sens[at, :])
        w_hi, w_lo = split(weighted[h, at, :])
        grad[h] += dot(s_hi, w_hi, tn) + dot(s_hi, w_lo, tn) + dot(s_lo, w_hi, tn)

    def smooth_part(step, h, q):
        @pl.when(q == 0)
        def _():
            halos(
                lambda i: halo(step, h, i, True).wait_send(),
                lambda i: halo(step, h, i, False).wait_send(),
            )
            halos(
                lambda i: halo(step, h, i, False).wait_recv(),
                lambda i: halo(step, h, i, True).wait_recv(),
            )

        base = q * prow + own
        inner = lax.rem(base, plane)
        first = base - inner
        cell = state[step, h, aligned(base, seg), :]
        total = jnp.zeros_like(cell)

        def add(other):
            diff = other - cell
            return diff / jnp.sqrt(1.0 + diff * diff)

        at = aligned(lax.rem(q, per_plane) * seg, seg)
        below = state[step, h, aligned(jnp.maximum(base - plane, 0), seg), :]
        above = state[step, h, aligned(jnp.minimum(base + plane, ncell - seg), seg), :]
        total += add(jnp.where(first == 0, under[step, h, at, :], below))
        total += add(jnp.where(first == ncell - plane, over[step, h, at, :], above))
        whole = pl.ds(pl.multiple_of(first, 16), plane)
        for k in range(4):
            column = near_ref[aligned(inner, seg), k:k + 1]
            pick = column == lax.broadcasted_iota(jnp.int32, (seg, plane), 1)
            pick = jnp.where(pick, 1.0, 0.0).astype(BF16)
            total += add(dot(pick, high[h, whole, :], nn) + dot(pick, low[h, whole, :], nn))
        scale = 1.0 - 0.75 * mask_ref[aligned(base, seg), :].astype(F32)
        smooth[h, aligned(q * seg, seg), :] = total * scale

    def at_slot(x, count, act):
        step, unit = lax.div(x, period), lax.rem(x, period)
        h, index = lax.div(unit, chunks), lax.rem(unit, chunks)

        @pl.when((x >= 0) & (step < ITERS) & (unit < units) & (index < count))
        def _():
            act(step, h, index)

    def cell_stage(s, step, h, c):
        def reweight(kept, total):
            misfit = total - obs[h, kept, :]
            weighted[h, kept, :] = misfit / jnp.maximum(jnp.abs(misfit), 1.0)

        cells.stage(s, c, h * chunks + c, part.at[h], land.at[h], weighted.at[h], reweight)

    def dp_stage(s, step, h, q):
        def update(kept, total):
            moved = state[step, h, kept, :] - 1.0 * total
            state[step + 1, h, kept, :] = moved + 0.05 * smooth[h, aligned(q * seg, seg), :]

        dp.stage(s, q, h * parts + q, grad.at[h], gland.at[h], state.at[step + 1, h], update)

    def slot(t, carry):
        @pl.when(t == 0)
        def _():
            for h in range(halves):
                watch(h).wait()

        for s in reversed(range(cells.stages + 1)):
            at_slot(t - LAG * s, chunks, functools.partial(cell_stage, s))
        for s in reversed(range(dp.stages + 1)):
            at_slot(t - delay - DP_LAG * s, parts, functools.partial(dp_stage, s))
        at_slot(t + 1, chunks, predict)
        at_slot(t - 2, parts, smooth_part)
        at_slot(t - LAG * cells.stages, chunks, back)
        return carry

    lax.fori_loop(-1, slots, slot, 0)
    for h in range(halves):
        leave(h).start()
    for h in range(halves):
        leave(h).wait()


def invert(n_dp, n_cells, sensitivity, observed, models, neighbour_map, edge_mask):
    ndata, ncell = sensitivity.shape
    width = models.shape[1] // HALVES
    plane = neighbour_map.shape[1]
    rows = max(CHUNK, 8 * n_cells)
    chunks = ndata // rows
    parts = ncell // plane * PARTS
    seg = ncell // parts // n_dp
    vmem = pl.BlockSpec(memory_space=pltpu.VMEM)
    hbm = pl.BlockSpec(memory_space=pl.ANY)
    dma = pltpu.SemaphoreType.DMA
    nd, nb = (2 * sum(d - 1 for d in digits) for digits in radix(n_dp, n_cells))
    return pl.pallas_call(
        functools.partial(body, (n_dp, n_cells), plane),
        out_shape=jax.ShapeDtypeStruct(models.shape, F32),
        in_specs=[hbm] * 3 + [vmem] * 2,
        out_specs=hbm,
        scratch_shapes=[
            pltpu.VMEM((ndata, ncell), F32),
            pltpu.VMEM((HALVES, ndata, width), F32),
            pltpu.VMEM((HALVES, ndata, width), F32),
            pltpu.VMEM((HALVES, ndata, width), F32),
            pltpu.VMEM((HALVES, ndata, width), F32),
            pltpu.VMEM((HALVES, ncell, width), F32),
            pltpu.VMEM((HALVES, ncell, width), F32),
            pltpu.VMEM((ITERS + 1, HALVES, ncell, width), F32),
            pltpu.VMEM((HALVES, ncell, width), BF16),
            pltpu.VMEM((HALVES, ncell, width), BF16),
            pltpu.VMEM((HALVES, parts * seg, width), F32),
            pltpu.VMEM((ITERS, HALVES, PARTS * seg, width), F32),
            pltpu.VMEM((ITERS, HALVES, PARTS * seg, width), F32),
            dma((chunks,)),
            dma((HALVES,)),
            dma((HALVES,)),
            dma((nb, HALVES * chunks)),
            dma((nb, HALVES * chunks)),
            dma((nd, HALVES * parts)),
            dma((nd, HALVES * parts)),
            dma((ITERS, HALVES, 2 * PARTS)),
            dma((ITERS, HALVES, 2 * PARTS)),
        ],
        compiler_params=pltpu.CompilerParams(
            collective_id=0, has_side_effects=True, vmem_limit_bytes=60 * 1024 * 1024
        ),
        name="invert",
    )(sensitivity, observed, models, neighbour_map.T, edge_mask[:, None])


def solution(mesh):
    return jax.shard_map(
        functools.partial(invert, mesh.shape["dp"], mesh.shape["cells"]),
        mesh=mesh,
        in_specs=(P("dp", "cells"), P("dp", None), P("cells", None), P(), P("cells")),
        out_specs=P("cells", None),
        check_vma=False,
    )
```
